256 devices in a mesh: nodes: 128 (over y, z, x), rep: 2 (over core).
Axes of the slice: x: 4, y: 4, z: 8, core: 2. Of those that a mesh axis runs over, the one named last changes fastest.
Arguments:
- node_latent: bfloat16 [40960, 512], P(('nodes', 'rep')), may hold values from -6 to 6
- edge_saved: bfloat16 [327680, 512], P(('nodes', 'rep')), may hold values from -6 to 6
- node_cot: bfloat16 [40960, 512], P(('nodes', 'rep')), may hold values from -6 to 6
- edge_cot: bfloat16 [327680, 512], P(('nodes', 'rep')), may hold values from -6 to 6
- senders: int32 [327680], P(('nodes', 'rep')), may hold values from 0 to 1343, as said below
- receivers: int32 [327680], P(('nodes', 'rep')), may hold values from 0 to 319
- ghost_rows: int32 [128, 128, 8], P('nodes'), may hold values from 0 to 319, as said below
- w_edge_in: bfloat16 [1536, 512], replicated, may hold values from -0.15625 to 0.15625
- w_edge_out: bfloat16 [512, 512], replicated, may hold values from -0.25 to 0.25
- edge_gain: float32 [512], replicated, may hold values from 0.5 to 2
- edge_offset: float32 [512], replicated, may hold values from -3 to 3
- w_node_in: bfloat16 [1024, 512], replicated, may hold values from -0.1875 to 0.1875
- w_node_out: bfloat16 [512, 512], replicated, may hold values from -0.25 to 0.25
- node_gain: float32 [512], replicated, may hold values from 0.5 to 2
Outputs:
- grad_nodes: bfloat16 [40960, 512], P(('nodes', 'rep'))
- grad_edges: bfloat16 [327680, 512], P(('nodes', 'rep'))
- grad_edge_in: bfloat16 [1536, 512], replicated
- grad_edge_out: bfloat16 [512, 512], replicated
- grad_node_in: bfloat16 [1024, 512], replicated
- grad_node_out: bfloat16 [512, 512], replicated
The draws below stay inside these ranges and needn't reach their ends.
Inputs may be any that keep to these rules, and one draw needn't show every extreme that they name: `senders`: A sender below 320 is a node of the edge's own partition; otherwise it is 320 + q * 8 + s, the ghost slot s of the list of a partition q other than the edge's own. Each list ghost_rows[q, p] holds 8 distinct rows.
All inputs are finite; a program needn't handle non-finite values.
Results may differ from the reference program's by a relative error of at most 0.008.
Values may be sent and summed in bfloat16 or wider, within the bound.
No kernel may reach another device: no remote copies, remote signals or barrier semaphores. Data moves between devices by JAX's collectives and lax.ppermute only.
A program may use at most 128 MiB of HBM per device.

```python
import math
import jax
import jax.numpy as jnp
from jax import lax

D = 512
NODE_PART = 320
GP = 8
PARTITIONS = 128
NODES = 40960
EDGES = 327680
N_REP = 2


def draw_senders(key, part):
    key_list = jax.random.split(jax.random.fold_in(key, 11), 5)
    edge_index = jnp.arange(EDGES, dtype=jnp.int32)
    own_part = edge_index // (EDGES // PARTITIONS)
    live_count = jax.random.randint(key_list[0], (PARTITIONS, PARTITIONS), 1, GP + 1)
    live_count = live_count.at[0, 1].set(GP)
    offset = jax.random.randint(key_list[1], (EDGES,), 1, PARTITIONS)
    source = (own_part + offset) % PARTITIONS
    slot_index = jax.random.randint(key_list[2], (EDGES,), 0, 1 << 20) % live_count[source, own_part]
    local_row = jax.random.randint(key_list[3], (EDGES,), 0, NODE_PART)
    remote = jax.random.randint(key_list[4], (EDGES,), 0, 2)
    return jnp.where(remote == 1, NODE_PART + source * GP + slot_index, local_row).astype(jnp.int32)


def draw_ghost_rows(key, part):
    key_list = jax.random.split(jax.random.fold_in(key, 23), PARTITIONS * PARTITIONS)
    picked = jax.vmap(lambda one_key: jax.random.permutation(one_key, NODE_PART)[:GP])(key_list)
    return picked.reshape(PARTITIONS, PARTITIONS, GP).astype(jnp.int32)


def touch_ends(array, rng, least, high):
    longest = array.shape.index(max(array.shape))
    spots = []
    for shift in (0, 1):
        where = [jax.random.randint(jax.random.fold_in(rng, axis), (), 0, length) for axis, length in enumerate(array.shape)]
        where[longest] = (where[longest] + shift) % array.shape[longest]
        spots.append(tuple(where))
    return array.at[spots[0]].set(least).at[spots[1]].set(high)


def block_levels(rng, shape, pieces, least, high):
    factor_of, own = 1.0, jax.random.fold_in(rng, 6)
    for dim, blocks in pieces:
        steps = jnp.exp(jax.random.uniform(jax.random.fold_in(own, dim), (blocks,), jnp.float32, least / len(pieces), high / len(pieces)))
        factor_of = factor_of * jnp.repeat(steps, shape[dim] // blocks).reshape([-1 if axis == dim else 1 for axis in range(len(shape))])
    return factor_of


def noise(stream_key, dims, spread, bound, cuts=(), kind=jnp.bfloat16):
    factor_of = block_levels(stream_key, dims, cuts, -0.22, 0.18) if cuts else 1.0
    array = jax.random.normal(stream_key, dims, jnp.float32) * spread * factor_of
    return jnp.minimum(jnp.maximum(array, -bound), bound).astype(kind)


def setup_inputs(seed: int = 0) -> dict:
    key_of = jax.random.split(jax.random.key(seed), 15)
    return {
        "node_latent": noise(key_of[0], (NODES, D), 1.0, 6.0, ((0, 256),)),
        "edge_saved": noise(key_of[1], (EDGES, D), 1.0, 6.0, ((0, 256),)),
        "node_cot": noise(key_of[2], (NODES, D), 1.0, 6.0, ((0, 256),)),
        "edge_cot": noise(key_of[3], (EDGES, D), 1.0, 6.0, ((0, 256),)),
        "senders": draw_senders(jax.random.fold_in(key_of[14], 71), 0),
        "receivers": touch_ends(jax.random.randint(key_of[5], (EDGES,), 0, NODE_PART), jax.random.fold_in(key_of[5], 1), 0, NODE_PART - 1).astype(jnp.int32),
        "ghost_rows": draw_ghost_rows(jax.random.fold_in(key_of[14], 71), 0),
        "w_edge_in": noise(key_of[7], (3 * D, D), (3 * D) ** -0.5, 0.15625),
        "w_edge_out": noise(key_of[8], (D, D), D ** -0.5, 0.25),
        "edge_gain": jnp.clip(jnp.exp(jax.random.uniform(key_of[9], (D,), jnp.float32, math.log(0.5), math.log(2.0))), 0.5, 2.0),
        "edge_offset": noise(key_of[10], (D,), 0.5, 3.0, (), jnp.float32),
        "w_node_in": noise(key_of[11], (2 * D, D), (2 * D) ** -0.5, 0.1875),
        "w_node_out": noise(key_of[12], (D, D), D ** -0.5, 0.25),
        "node_gain": jnp.clip(jnp.exp(jax.random.uniform(key_of[13], (D,), jnp.float32, math.log(0.5), math.log(2.0))), 0.5, 2.0),
    }


EPS = 1e-05

def mat_mul(left, right):
    return jnp.dot(left, right, preferred_element_type=jnp.float32)

def mat_tn(left, right):
    return lax.dot_general(left, right, (((0,), (0,)), ((), ())), preferred_element_type=jnp.float32)

def mat_nt(left, right):
    return lax.dot_general(left, right, (((1,), (1,)), ((), ())), preferred_element_type=jnp.float32)

def silu_slope(value):
    sigmoid_v = jax.nn.sigmoid(value)
    return sigmoid_v * (1.0 + value * (1.0 - sigmoid_v))

def norm_forward(value):
    centred = value - lax.optimization_barrier(jnp.mean(value, axis=-1, keepdims=True))
    inverse = lax.rsqrt(lax.optimization_barrier(jnp.mean(centred * centred, axis=-1, keepdims=True)) + EPS)
    return (centred * inverse, inverse)

def norm_backward(grad_hat, normed, inverse):
    return inverse * (grad_hat - lax.optimization_barrier(jnp.mean(grad_hat, axis=-1, keepdims=True)) - normed * lax.optimization_barrier(jnp.mean(grad_hat * normed, axis=-1, keepdims=True)))

def edge_forward(edge_block, send_rows, recv_rows, w_edge_in, w_edge_out, edge_gain, edge_offset):
    latent_width = edge_block.shape[1]
    pre_act = mat_mul(edge_block, w_edge_in[:latent_width]) + mat_mul(send_rows, w_edge_in[latent_width:2 * latent_width]) + mat_mul(recv_rows, w_edge_in[2 * latent_width:])
    edge_hidden = jax.nn.silu(pre_act).astype(jnp.bfloat16)
    edge_normed, edge_inverse = norm_forward(mat_mul(edge_hidden, w_edge_out))
    message = edge_normed * edge_gain + edge_offset
    return (pre_act, edge_hidden, edge_normed, edge_inverse, message)

def edge_backward(edge_block, send_rows, recv_rows, edge_cot, message_grad, saved, w_edge_in, w_edge_out, edge_gain):
    pre_act, edge_hidden, edge_normed, edge_inverse = saved
    latent_width = edge_block.shape[1]
    grad_out = norm_backward(message_grad * edge_gain, edge_normed, edge_inverse).astype(jnp.bfloat16)
    grad_act = (mat_nt(grad_out, w_edge_out) * silu_slope(pre_act)).astype(jnp.bfloat16)
    in_grad = jnp.concatenate([mat_tn(edge_block, grad_act), mat_tn(send_rows, grad_act), mat_tn(recv_rows, grad_act)], 0)
    out_grad = mat_tn(edge_hidden, grad_out)
    edge_grad = (edge_cot.astype(jnp.float32) + mat_nt(grad_act, w_edge_in[:latent_width])).astype(jnp.bfloat16)
    send_grad = mat_nt(grad_act, w_edge_in[latent_width:2 * latent_width])
    recv_grad = mat_nt(grad_act, w_edge_in[2 * latent_width:])
    return (edge_grad, send_grad, recv_grad, in_grad, out_grad)

def node_pass(node_rows, totals_b, node_cot, w_node_in, w_node_out, node_gain):
    latent_width = node_rows.shape[1]
    node_pre = mat_mul(node_rows, w_node_in[:latent_width]) + mat_mul(totals_b, w_node_in[latent_width:])
    node_hidden = jax.nn.silu(node_pre).astype(jnp.bfloat16)
    node_normed, node_inverse = norm_forward(mat_mul(node_hidden, w_node_out))
    grad_out = norm_backward(node_cot.astype(jnp.float32) * node_gain, node_normed, node_inverse).astype(jnp.bfloat16)
    grad_act = (mat_nt(grad_out, w_node_out) * silu_slope(node_pre)).astype(jnp.bfloat16)
    in_grad = jnp.concatenate([mat_tn(node_rows, grad_act), mat_tn(totals_b, grad_act)], 0)
    direct_grad = mat_nt(grad_act, w_node_in[:latent_width])
    totals_grad = mat_nt(grad_act, w_node_in[latent_width:]).astype(jnp.bfloat16)
    return (direct_grad, totals_grad, in_grad, mat_tn(node_hidden, grad_out))

def reference(node_latent, edge_saved, node_cot, edge_cot, senders, receivers, ghost_rows, w_edge_in, w_edge_out, edge_gain, edge_offset, w_node_in, w_node_out, node_gain):
    latent_width = node_latent.shape[1]
    part_count = ghost_rows.shape[0]
    part_rows = node_latent.shape[0] // part_count
    part_edges = senders.shape[0] // part_count
    edge_latent = jnp.flip(edge_saved.reshape(part_count, N_REP, part_edges // N_REP, latent_width), axis=1).reshape(edge_saved.shape)
    global_ghost = (jnp.arange(part_count, dtype=jnp.int32)[:, None, None] * part_rows + ghost_rows).astype(jnp.int32)
    zero_sums = (jnp.zeros(w_edge_in.shape, jnp.float32), jnp.zeros(w_edge_out.shape, jnp.float32), jnp.zeros(w_node_in.shape, jnp.float32), jnp.zeros(w_node_out.shape, jnp.float32))

    def one_part(state_carry, part_index):
        grad_nodes, weight_sums = state_carry
        row_start = (part_index * part_rows).astype(jnp.int32)
        edge_start = (part_index * part_edges).astype(jnp.int32)
        part_latent = lax.dynamic_slice_in_dim(node_latent, row_start, part_rows, 0)
        ghost_index = lax.dynamic_index_in_dim(global_ghost, part_index, 1, keepdims=False).reshape(-1)
        node_table = jnp.concatenate([part_latent, node_latent[ghost_index]], 0)
        edge_block = lax.dynamic_slice_in_dim(edge_latent, edge_start, part_edges, 0)
        sender_block = lax.dynamic_slice_in_dim(senders, edge_start, part_edges, 0)
        receiver_block = lax.dynamic_slice_in_dim(receivers, edge_start, part_edges, 0)
        cot_block = lax.dynamic_slice_in_dim(edge_cot, edge_start, part_edges, 0)
        node_cot_block = lax.dynamic_slice_in_dim(node_cot, row_start, part_rows, 0)
        send_rows = node_table[sender_block]
        recv_rows = part_latent[receiver_block]
        pre_act, edge_hidden, edge_normed, edge_inverse, message = edge_forward(edge_block, send_rows, recv_rows, w_edge_in, w_edge_out, edge_gain, edge_offset)
        totals = jax.ops.segment_sum(message, receiver_block, num_segments=part_rows)
        direct_grad, totals_grad, node_in_grad, node_out_grad = node_pass(part_latent, totals.astype(jnp.bfloat16), node_cot_block, w_node_in, w_node_out, node_gain)
        message_grad = cot_block.astype(jnp.float32) + totals_grad[receiver_block].astype(jnp.float32)
        edge_grad, send_grad, recv_grad, edge_in_grad, edge_out_grad = edge_backward(edge_block, send_rows, recv_rows, cot_block, message_grad, (pre_act, edge_hidden, edge_normed, edge_inverse), w_edge_in, w_edge_out, edge_gain)
        table_grad = jax.ops.segment_sum(send_grad, sender_block, num_segments=part_rows + ghost_index.shape[0])
        row_grad = table_grad[:part_rows] + jax.ops.segment_sum(recv_grad, receiver_block, num_segments=part_rows) + direct_grad + node_cot_block.astype(jnp.float32)
        grad_nodes = grad_nodes.at[ghost_index].add(table_grad[part_rows:])
        grad_nodes = lax.dynamic_update_slice_in_dim(grad_nodes, lax.dynamic_slice_in_dim(grad_nodes, row_start, part_rows, 0) + row_grad, row_start, 0)
        weight_sums = (weight_sums[0] + edge_in_grad, weight_sums[1] + edge_out_grad, weight_sums[2] + node_in_grad, weight_sums[3] + node_out_grad)
        return ((grad_nodes, weight_sums), edge_grad)
    start_nodes = jnp.zeros(node_latent.shape, jnp.float32)
    (grad_nodes, weight_sums), edge_grads = lax.scan(one_part, (start_nodes, zero_sums), jnp.arange(part_count, dtype=jnp.int32))
    edge_scale = 1.0 / math.sqrt(EDGES)
    node_scale = 1.0 / math.sqrt(NODES)
    return (grad_nodes.astype(jnp.bfloat16), edge_grads.reshape(edge_saved.shape), (weight_sums[0] * edge_scale).astype(jnp.bfloat16), (weight_sums[1] * edge_scale).astype(jnp.bfloat16), (weight_sums[2] * node_scale).astype(jnp.bfloat16), (weight_sums[3] * node_scale).astype(jnp.bfloat16))
```

```python
import math

import jax
import jax.numpy as jnp
from jax import lax
from jax.sharding import PartitionSpec as P

EPS = 1e-05
bf16 = jnp.bfloat16
f32 = jnp.float32


def swapped(array):
    pairs = [(i, 1 - i) for i in range(2)]
    return lax.ppermute(array, "rep", pairs)


def mat_mul(left, right):
    return jnp.dot(left, right, preferred_element_type=f32)


def mat_tn(left, right):
    return lax.dot_general(left, right, (((0,), (0,)), ((), ())), preferred_element_type=f32)


def mat_nt(left, right):
    return lax.dot_general(left, right, (((1,), (1,)), ((), ())), preferred_element_type=f32)


def split_two(value):
    high = lax.reduce_precision(value, 8, 7)
    return high.astype(bf16), (value - high).astype(bf16)


def silu_slope(value):
    sigmoid_v = jax.nn.sigmoid(value)
    return sigmoid_v * (1.0 + value * (1.0 - sigmoid_v))


def norm_forward(value):
    centred = value - jnp.mean(value, axis=-1, keepdims=True)
    inverse = lax.rsqrt(jnp.mean(centred * centred, axis=-1, keepdims=True) + EPS)
    return (centred * inverse, inverse)


def norm_backward(grad_hat, normed, inverse):
    return inverse * (
        grad_hat
        - jnp.mean(grad_hat, axis=-1, keepdims=True)
        - normed * jnp.mean(grad_hat * normed, axis=-1, keepdims=True)
    )


def one_hot(index, width):
    return (index[:, None] == lax.broadcasted_iota(jnp.int32, (1, width), 1)).astype(bf16)


def reduce_groups(sizes):
    ny, nz, nx = sizes

    def device(y, z, x, r):
        return ((y * nz + z) * nx + x) * 2 + r

    near = [[device(y, z, x, 0) for x in range(nx)] for y in range(ny) for z in range(nz)]
    near += [[device(y, z, x, 1) for y in range(ny)] for x in range(nx) for z in range(nz)]
    far = [[device(y, z, x, 0) for y in range(ny) for z in range(nz)] for x in range(nx)]
    far += [[device(y, z, x, 1) for x in range(nx) for z in range(nz)] for y in range(ny)]
    return near, far


def exchange(array, groups):
    return lax.all_to_all(
        array, ("nodes", "rep"), 0, 0, tiled=True, axis_index_groups=groups
    )


def total_over_devices(weight_grads, core):
    near, far = reduce_groups((4, 8, 4))
    rows, width = weight_grads.shape
    half = rows // 2
    kept = lax.dynamic_slice_in_dim(weight_grads, core * half, half, 0)
    sent = lax.dynamic_slice_in_dim(weight_grads, (1 - core) * half, half, 0).astype(bf16)
    pair = (kept + swapped(sent).astype(f32)).astype(bf16)
    n_near, n_far = len(near[0]), len(far[0])
    blocks = exchange(pair.reshape(n_near, half // n_near, width), near)
    part = jnp.sum(blocks.astype(f32), axis=0).astype(bf16)
    rows_far = half // n_near // n_far
    blocks = exchange(part.reshape(n_far, rows_far, width), far)
    part = jnp.sum(blocks.astype(f32), axis=0).astype(bf16)
    part = exchange(jnp.broadcast_to(part[None], (n_far, rows_far, width)), far)
    part = part.reshape(half // n_near, width)
    part = exchange(jnp.broadcast_to(part[None], (n_near, half // n_near, width)), near)
    return lax.all_gather(part.reshape(half, width), "rep", axis=0, tiled=True)


def shards(
    node_latent,
    edge_saved,
    node_cot,
    edge_cot,
    senders,
    receivers,
    ghost_rows,
    w_edge_in,
    w_edge_out,
    edge_gain,
    edge_offset,
    w_node_in,
    w_node_out,
    node_gain,
):
    width = node_latent.shape[1]
    own = node_latent.shape[0]
    rows = 2 * own
    core = lax.axis_index("rep")
    slots = ghost_rows.shape[2] // 2
    parts = ghost_rows.shape[1]
    ghosts = parts * slots

    def local_row(index):
        moved = index - core * own
        return jnp.where(moved < 0, moved + rows, moved)

    partition = jnp.concatenate([node_latent, swapped(node_latent)], 0)
    lists = lax.dynamic_slice_in_dim(ghost_rows[0], core * slots, slots, 1).reshape(-1)
    pick_ghost = one_hot(local_row(lists), rows)
    outgoing = mat_mul(pick_ghost, partition).astype(bf16)
    arrived = lax.all_to_all(outgoing, "nodes", 0, 0, tiled=True)

    edge_latent = swapped(edge_saved)
    node_cots = jnp.concatenate([node_cot, swapped(node_cot)], 0)
    pick_recv = one_hot(local_row(receivers), rows)
    pick_local = one_hot(jnp.where(senders < rows, local_row(senders), -1), rows)
    slot = senders - rows
    side = ((slot >> 2) & 1) ^ core
    ghost_index = jnp.where(
        slot >= 0, side * ghosts + (slot >> 3) * slots + (slot & (slots - 1)), -1
    )
    pick_sent = one_hot(ghost_index, 2 * ghosts)
    recv_rows = mat_mul(pick_recv, partition).astype(bf16)
    local_rows = mat_mul(pick_local, partition)
    a1, a2, a3 = w_edge_in[:width], w_edge_in[width : 2 * width], w_edge_in[2 * width :]
    known = mat_mul(edge_latent, a1) + mat_mul(recv_rows, a3)

    ghost_table = jnp.concatenate([arrived, swapped(arrived)], 0)
    send_rows = (local_rows + mat_mul(pick_sent, ghost_table)).astype(bf16)
    pre_act = known + mat_mul(send_rows, a2)
    edge_hidden = jax.nn.silu(pre_act).astype(bf16)
    edge_normed, edge_inverse = norm_forward(mat_mul(edge_hidden, w_edge_out))
    message = edge_normed * edge_gain + edge_offset
    high, low = split_two(message)
    partial = mat_tn(pick_recv, high) + mat_tn(pick_recv, low)
    totals = (partial + jnp.roll(swapped(partial), own, 0)).astype(bf16)

    b1, b2 = w_node_in[:width], w_node_in[width:]
    node_pre = mat_mul(partition, b1) + mat_mul(totals, b2)
    node_hidden = jax.nn.silu(node_pre).astype(bf16)
    node_normed, node_inverse = norm_forward(mat_mul(node_hidden, w_node_out))
    node_grad_out = norm_backward(
        node_cots.astype(f32) * node_gain, node_normed, node_inverse
    ).astype(bf16)
    node_grad_act = (mat_nt(node_grad_out, w_node_out) * silu_slope(node_pre)).astype(bf16)
    totals_grad = mat_nt(node_grad_act, b2).astype(bf16)
    direct_grad = mat_nt(node_grad_act[:own], b1)

    message_grad = edge_cot.astype(f32) + mat_mul(pick_recv, totals_grad)
    edge_grad_out = norm_backward(
        message_grad * edge_gain, edge_normed, edge_inverse
    ).astype(bf16)
    edge_grad_act = (mat_nt(edge_grad_out, w_edge_out) * silu_slope(pre_act)).astype(bf16)
    grad_edges = (edge_cot.astype(f32) + mat_nt(edge_grad_act, a1)).astype(bf16)

    sent_sum = mat_tn(pick_sent, edge_grad_act)
    paired = (sent_sum[:ghosts] + swapped(sent_sum[ghosts:].astype(bf16)).astype(f32)).astype(bf16)
    returned = lax.all_to_all(paired, "nodes", 0, 0, tiled=True)

    device_count = lax.axis_size("nodes") * lax.axis_size("rep")
    edge_scale = 1.0 / math.sqrt(senders.shape[0] * device_count)
    node_scale = 1.0 / math.sqrt(own * device_count)
    weight_grads = jnp.concatenate(
        [
            mat_tn(edge_latent, edge_grad_act) * edge_scale,
            mat_tn(send_rows, edge_grad_act) * edge_scale,
            mat_tn(recv_rows, edge_grad_act) * edge_scale,
            mat_tn(edge_hidden, edge_grad_out) * edge_scale,
            mat_tn(node_latent, node_grad_act[:own]) * node_scale,
            mat_tn(totals[:own], node_grad_act[:own]) * node_scale,
            mat_tn(node_hidden[:own], node_grad_out[:own]) * node_scale,
        ],
        0,
    )

    send_high, send_low = split_two(mat_tn(pick_local, edge_grad_act) + mat_tn(pick_ghost, returned))
    recv_high, recv_low = split_two(mat_tn(pick_recv, edge_grad_act))
    row_grad = (
        mat_nt(recv_high, a3) + mat_nt(recv_low, a3) + mat_nt(send_high, a2) + mat_nt(send_low, a2)
    )
    own_grad = row_grad[:own] + swapped(row_grad[own:])
    grad_nodes = (own_grad + direct_grad + node_cot.astype(f32)).astype(bf16)

    total = total_over_devices(weight_grads, core)
    return (
        grad_nodes,
        grad_edges,
        total[: 3 * width],
        total[3 * width : 4 * width],
        total[4 * width : 6 * width],
        total[6 * width :],
    )


def solution(mesh):
    rows = P(("nodes", "rep"), None)
    flat = P(("nodes", "rep"))
    return jax.shard_map(
        shards,
        mesh=mesh,
        in_specs=(rows, rows, rows, rows, flat, flat, P("nodes", None, None)) + (P(),) * 7,
        out_specs=(rows, rows, P(), P(), P(), P()),
        check_vma=False,
    )
```

```python
import functools
import math

import jax
import jax.numpy as jnp
from jax import lax
from jax.experimental import pallas as pl
from jax.experimental.pallas import tpu as pltpu
from jax.sharding import PartitionSpec as P

EPS = 1e-05
bf16 = jnp.bfloat16
f32 = jnp.float32


def swapped(array):
    pairs = [(i, 1 - i) for i in range(2)]
    return lax.ppermute(array, "rep", pairs)


def mat_mul(left, right):
    return jnp.dot(left, right, preferred_element_type=f32)


def mat_tn(left, right):
    return lax.dot_general(left, right, (((0,), (0,)), ((), ())), preferred_element_type=f32)


def mat_nt(left, right):
    return lax.dot_general(left, right, (((1,), (1,)), ((), ())), preferred_element_type=f32)


def split_two(value):
    high = lax.reduce_precision(value, 8, 7)
    return high.astype(bf16), (value - high).astype(bf16)


def silu_slope(value):
    sigmoid_v = jax.nn.sigmoid(value)
    return sigmoid_v * (1.0 + value * (1.0 - sigmoid_v))


def norm_forward(value):
    centred = value - jnp.mean(value, axis=-1, keepdims=True)
    inverse = lax.rsqrt(jnp.mean(centred * centred, axis=-1, keepdims=True) + EPS)
    return (centred * inverse, inverse)


def norm_backward(grad_hat, normed, inverse):
    return inverse * (
        grad_hat
        - jnp.mean(grad_hat, axis=-1, keepdims=True)
        - normed * jnp.mean(grad_hat * normed, axis=-1, keepdims=True)
    )


def one_hot(index, width):
    return (index[:, None] == lax.broadcasted_iota(jnp.int32, (1, width), 1)).astype(bf16)


def groups(sizes):
    ny, nz, nx = sizes

    def device(y, z, x, r):
        return ((y * nz + z) * nx + x) * 2 + r

    near = [[device(y, z, x, 0) for x in range(nx)] for y in range(ny) for z in range(nz)]
    near += [[device(y, z, x, 1) for y in range(ny)] for x in range(nx) for z in range(nz)]
    far = [[device(y, z, x, 0) for y in range(ny) for z in range(nz)] for x in range(nx)]
    far += [[device(y, z, x, 1) for x in range(nx) for z in range(nz)] for y in range(ny)]
    return near, far


NEAR, FAR = groups((4, 8, 4))


def exchange(array, stage):
    return lax.all_to_all(array, ("nodes", "rep"), 0, 0, tiled=True, axis_index_groups=stage)


def summed(value, stage):
    count = len(stage[0])
    blocks = exchange(value.reshape(count, value.shape[0] // count, value.shape[1]), stage)
    return jnp.sum(blocks.astype(f32), axis=0).astype(bf16)


def gathered(value, stage):
    count = len(stage[0])
    blocks = exchange(jnp.broadcast_to(value[None], (count, *value.shape)), stage)
    return blocks.reshape(count * value.shape[0], value.shape[1])


def reduced(kept, sent, core):
    value = (kept + swapped(sent).astype(f32)).astype(bf16)
    return summed(summed(value, NEAR), FAR)


def spread(value, core):
    value = gathered(gathered(value, FAR), NEAR)
    width = value.shape[1]
    return assemble(value, swapped(value), core, [3 * width, width, 2 * width, width])


def assemble_kernel(sizes, core_ref, mine_ref, got_ref, *refs):
    outs, sems = refs[:-1], refs[-1]
    core = core_ref[0]
    copies = []
    start = 0
    half = mine_ref.shape[1] // 2
    for k, rows in enumerate(sizes):
        for block in range(rows // (2 * half)):
            for source, place in ((mine_ref, core), (got_ref, 1 - core)):
                row = pl.multiple_of(block * 2 * half + place * half, half)
                copies.append(
                    pltpu.make_async_copy(
                        source.at[pl.ds(start, half), :],
                        outs[k].at[pl.ds(row, half), :],
                        sems.at[len(copies)],
                    )
                )
            start += half
    for copy in copies:
        copy.start()
    for copy in copies:
        copy.wait()


def assemble(mine, got, core, sizes):
    return pl.pallas_call(
        functools.partial(assemble_kernel, sizes),
        out_shape=[jax.ShapeDtypeStruct((rows, mine.shape[1]), mine.dtype) for rows in sizes],
        in_specs=[pl.BlockSpec(memory_space=pltpu.SMEM)]
        + [pl.BlockSpec(memory_space=pltpu.VMEM)] * 2,
        out_specs=[pl.BlockSpec(memory_space=pl.ANY)] * len(sizes),
        scratch_shapes=[pltpu.SemaphoreType.DMA((14,))],
        name="assemble",
    )(core.astype(jnp.int32).reshape(1), mine, got)


CHUNK = 1280


def by_lane(index, count):
    return (index == lax.broadcasted_iota(jnp.int32, (index.shape[0], count), 1)).astype(bf16)


def by_row(index, count):
    return (index == lax.broadcasted_iota(jnp.int32, (count, index.shape[1]), 0)).astype(bf16)


def in_two(value):
    high = value.astype(bf16)
    return high, (value - high.astype(f32)).astype(bf16)


def silu_parts(value):
    sigmoid_v = 1.0 / (1.0 + jnp.exp(-value))
    return value * sigmoid_v, sigmoid_v * (1.0 + value * (1.0 - sigmoid_v))


def each_chunk(count, body):
    def step(i, carry):
        body(pl.ds(pl.multiple_of(i * CHUNK, CHUNK), CHUNK))
        return carry

    lax.fori_loop(0, count // CHUNK, step, 0)


def forward_kernel(
    known_ref, local_ref, send_col_ref, recv_row_ref, mine_ref, theirs_ref, w_in_ref, w_out_ref, gain_ref,
    offset_ref, send_ref, slope_ref, hidden_ref, normed_ref, inverse_ref, totals_ref, high_ref, low_ref,
    table_ref,
):
    width = known_ref.shape[1]
    ghosts = mine_ref.shape[0]
    table_ref[:ghosts] = mine_ref[...]
    table_ref[ghosts:] = theirs_ref[...]
    count = totals_ref.shape[0]

    def body(at):
        index = send_col_ref[at] - count
        rows = mat_mul(by_lane(index, 2 * ghosts), table_ref[...])
        send_rows = (local_ref[at].astype(f32) + rows).astype(bf16)
        send_ref[at] = send_rows
        pre_act = known_ref[at] + mat_mul(send_rows, w_in_ref[width : 2 * width])
        hidden, slope = silu_parts(pre_act)
        slope_ref[at] = slope
        hidden = hidden.astype(bf16)
        hidden_ref[at] = hidden
        normed, inverse = norm_forward(mat_mul(hidden, w_out_ref[...]))
        normed_ref[at] = normed
        inverse_ref[at] = jnp.broadcast_to(inverse, (CHUNK, inverse_ref.shape[1]))
        high, low = in_two(normed * gain_ref[...] + offset_ref[...])
        high_ref[at] = high
        low_ref[at] = low

    each_chunk(known_ref.shape[0], body)
    pick = by_row(recv_row_ref[...], count)
    totals_ref[...] = mat_mul(pick, high_ref[...]) + mat_mul(pick, low_ref[...])


def backward_kernel(
    partial_ref, other_ref, part_ref, node_cot_ref, w_node_in_ref, w_node_out_ref, node_gain_ref,
    cot_ref, slope_ref, normed_ref, inverse_ref,
    recv_col_ref, send_row_ref, w_out_ref, gain_ref,
    theirs_ref, mine_ref, grad_act_ref, grad_out_ref,
    totals_ref, node_hidden_ref, node_act_ref, node_out_ref,
    totals_grad_ref,
):
    width = cot_ref.shape[1]
    rows = part_ref.shape[0]
    own = rows // 2
    ghosts = mine_ref.shape[0]
    totals = jnp.concatenate(
        [partial_ref[:own] + other_ref[own:], partial_ref[own:] + other_ref[:own]], 0
    ).astype(bf16)
    node_pre = mat_mul(part_ref[...], w_node_in_ref[:width]) + mat_mul(
        totals, w_node_in_ref[width:]
    )
    hidden, slope = silu_parts(node_pre)
    hidden = hidden.astype(bf16)
    normed, inverse = norm_forward(mat_mul(hidden, w_node_out_ref[...]))
    grad_out = norm_backward(
        node_cot_ref[...].astype(f32) * node_gain_ref[...], normed, inverse
    ).astype(bf16)
    grad_act = (mat_nt(grad_out, w_node_out_ref[...]) * slope).astype(bf16)
    totals_grad_ref[...] = mat_nt(grad_act, w_node_in_ref[width:]).astype(bf16)
    totals_ref[...] = totals[:own]
    node_hidden_ref[...] = hidden[:own]
    node_act_ref[...] = grad_act[:own]
    node_out_ref[...] = grad_out[:own]

    def body(at):
        message_grad = cot_ref[at].astype(f32) + mat_mul(
            by_lane(recv_col_ref[at], rows), totals_grad_ref[...]
        )
        grad_out = norm_backward(
            message_grad * gain_ref[...], normed_ref[at], inverse_ref[at][:, :1]
        ).astype(bf16)
        grad_out_ref[at] = grad_out
        grad_act_ref[at] = (mat_nt(grad_out, w_out_ref[...]) * slope_ref[at]).astype(bf16)

    each_chunk(cot_ref.shape[0], body)
    index = send_row_ref[...]
    theirs_ref[...] = mat_mul(by_row(index - rows - ghosts, ghosts), grad_act_ref[...]).astype(bf16)
    mine_ref[...] = mat_mul(by_row(index - rows, ghosts), grad_act_ref[...])


def weights_kernel(
    core_ref, edge_ref, send_ref, recv_ref, hidden_ref, part_ref, totals_ref, node_hidden_ref,
    grad_act_ref, grad_out_ref, node_act_ref, node_out_ref, cot_ref, w_in_ref,
    recv_row_ref, send_row_ref, node_cot_ref, w_node_in_ref,
    kept_ref, sent_ref, grad_edge_ref, local_ref, recv_sum_ref, direct_ref, block_ref,
    *, edge_scale, node_scale,
):
    width = edge_ref.shape[1]
    half = width // 2
    core = core_ref[0]
    own = totals_ref.shape[0]
    products = [
        (edge_ref[...], grad_act_ref[...], edge_scale),
        (send_ref[...], grad_act_ref[...], edge_scale),
        (recv_ref[...], grad_act_ref[...], edge_scale),
        (hidden_ref[...], grad_out_ref[...], edge_scale),
        (part_ref[:own], node_act_ref[...], node_scale),
        (totals_ref[...], node_act_ref[...], node_scale),
        (node_hidden_ref[...], node_out_ref[...], node_scale),
    ]
    for k, (left, right, scale) in enumerate(products):
        block_ref[...] = mat_tn(left, right) * scale
        mine = block_ref[pl.ds(pl.multiple_of(core * half, half), half), :]
        other = block_ref[pl.ds(pl.multiple_of((1 - core) * half, half), half), :]
        kept_ref[k * half : (k + 1) * half] = mine
        sent_ref[k * half : (k + 1) * half] = other.astype(bf16)

    def body(at):
        grad_edge_ref[at] = (
            cot_ref[at].astype(f32) + mat_nt(grad_act_ref[at], w_in_ref[:width])
        ).astype(bf16)

    each_chunk(cot_ref.shape[0], body)
    rows = part_ref.shape[0]
    local_ref[...] = mat_mul(by_row(send_row_ref[...], rows), grad_act_ref[...])
    recv_sum_ref[...] = mat_mul(by_row(recv_row_ref[...], rows), grad_act_ref[...])
    direct_ref[...] = mat_nt(node_act_ref[...], w_node_in_ref[:width]) + node_cot_ref[...].astype(f32)


def run(kernel, name, arguments, results, scratch=(), scalars=0, flops=0):
    vmem = pl.BlockSpec(memory_space=pltpu.VMEM)
    return pl.pallas_call(
        kernel,
        in_specs=[pl.BlockSpec(memory_space=pltpu.SMEM)] * scalars
        + [vmem] * (len(arguments) - scalars),
        out_specs=[vmem] * len(results),
        out_shape=[jax.ShapeDtypeStruct(*result) for result in results],
        scratch_shapes=list(scratch),
        compiler_params=pltpu.CompilerParams(vmem_limit_bytes=60 * 1024 * 1024),
        cost_estimate=pl.CostEstimate(
            flops=flops, transcendentals=0, bytes_accessed=8 * 1024 * 1024
        ),
        name=name,
    )(*arguments)


def shards(
    node_latent,
    edge_saved,
    node_cot,
    edge_cot,
    senders,
    receivers,
    ghost_rows,
    w_edge_in,
    w_edge_out,
    edge_gain,
    edge_offset,
    w_node_in,
    w_node_out,
    node_gain,
):
    width = node_latent.shape[1]
    own = node_latent.shape[0]
    rows = 2 * own
    core = lax.axis_index("rep")
    slots = ghost_rows.shape[2] // 2
    parts = ghost_rows.shape[1]
    ghosts = parts * slots

    def local_row(index):
        moved = index - core * own
        return jnp.where(moved < 0, moved + rows, moved)

    partition = jnp.concatenate([node_latent, swapped(node_latent)], 0)
    lists = lax.dynamic_slice_in_dim(ghost_rows[0], core * slots, slots, 1).reshape(-1)
    pick_ghost = one_hot(local_row(lists), rows)
    outgoing = mat_mul(pick_ghost, partition).astype(bf16)
    arrived = lax.all_to_all(outgoing.reshape(parts, slots, width), "nodes", 0, 0, tiled=True)

    edge_latent = swapped(edge_saved)
    node_cots = jnp.concatenate([node_cot, swapped(node_cot)], 0)
    edges = senders.shape[0]
    receiver = local_row(receivers)
    slot = senders - rows
    side = ((slot >> 2) & 1) ^ core
    sender = jnp.where(
        slot >= 0,
        rows + side * ghosts + (slot >> 3) * slots + (slot & (slots - 1)),
        local_row(senders),
    )
    recv_col, send_col = receiver[:, None], sender[:, None]
    recv_row, send_row = receiver[None], sender[None]
    square = 2 * edges * width * width
    pick_recv = one_hot(receiver, rows)
    pick_local = one_hot(jnp.where(slot >= 0, -1, sender), rows)
    recv_rows = mat_mul(pick_recv, partition).astype(bf16)
    local_rows = mat_mul(pick_local, partition).astype(bf16)
    known = mat_mul(edge_latent, w_edge_in[:width]) + mat_mul(recv_rows, w_edge_in[2 * width :])
    arrived, known, local_rows, recv_rows, recv_col, send_col = lax.optimization_barrier(
        (arrived, known, local_rows, recv_rows, recv_col, send_col)
    )
    arrived = arrived.reshape(ghosts, width)
    send_rows, edge_slope, edge_hidden, edge_normed, edge_inverse, partial = run(
        forward_kernel,
        "forward",
        [
            known,
            local_rows,
            send_col,
            recv_row,
            arrived,
            swapped(arrived),
            w_edge_in,
            w_edge_out,
            edge_gain[None],
            edge_offset[None],
        ],
        [
            ((edges, width), bf16),
            ((edges, width), f32),
            ((edges, width), bf16),
            ((edges, width), f32),
            ((edges, 128), f32),
            ((rows, width), f32),
        ],
        [pltpu.VMEM((edges, width), bf16)] * 2 + [pltpu.VMEM((2 * ghosts, width), bf16)],
        flops=6 * square,
    )
    device_count = lax.axis_size("nodes") * lax.axis_size("rep")
    edge_scale = 1.0 / math.sqrt(edges * device_count)
    node_scale = 1.0 / math.sqrt(own * device_count)
    (
        theirs, mine, grad_act, grad_out,
        totals, node_hidden, node_act, node_out,
    ) = run(
        backward_kernel,
        "backward",
        [
            partial,
            swapped(partial),
            partition,
            node_cots,
            w_node_in,
            w_node_out,
            node_gain[None],
            edge_cot,
            edge_slope,
            edge_normed,
            edge_inverse,
            recv_col,
            send_row,
            w_edge_out,
            edge_gain[None],
        ],
        [
            ((ghosts, width), bf16),
            ((ghosts, width), f32),
            ((edges, width), bf16),
            ((edges, width), bf16),
        ]
        + [((own, width), bf16)] * 4,
        [pltpu.VMEM((rows, width), bf16)],
        flops=8 * square,
    )
    paired = (mine + swapped(theirs).astype(f32)).astype(bf16)
    paired, grad_act = lax.optimization_barrier((paired, grad_act))
    returned = lax.all_to_all(paired.reshape(parts, slots, width), "nodes", 0, 0, tiled=True)

    kept, sent, grad_edges, local_sum, recv_sum, direct_grad = run(
        functools.partial(weights_kernel, edge_scale=edge_scale, node_scale=node_scale),
        "weights",
        [
            core.astype(jnp.int32).reshape(1),
            edge_latent,
            send_rows,
            recv_rows,
            edge_hidden,
            partition,
            totals,
            node_hidden,
            grad_act,
            grad_out,
            node_act,
            node_out,
            edge_cot,
            w_edge_in,
            recv_row,
            send_row,
            node_cot,
            w_node_in,
        ],
        [((7 * width // 2, width), f32), ((7 * width // 2, width), bf16), ((edges, width), bf16)]
        + [((rows, width), f32)] * 2
        + [((own, width), f32)],
        [pltpu.VMEM((width, width), f32)],
        scalars=1,
        flops=6 * square,
    )

    kept, sent, returned = lax.optimization_barrier((kept, sent, returned))
    value = reduced(kept, sent, core)
    send_high, send_low = split_two(local_sum + mat_tn(pick_ghost, returned.reshape(ghosts, width)))
    recv_high, recv_low = split_two(recv_sum)
    a2, a3 = w_edge_in[width : 2 * width], w_edge_in[2 * width :]
    row_grad = (
        mat_nt(recv_high, a3) + mat_nt(recv_low, a3) + mat_nt(send_high, a2) + mat_nt(send_low, a2)
    )
    own_grad = row_grad[:own] + swapped(row_grad[own:])
    grad_nodes = (own_grad + direct_grad).astype(bf16)

    value, grad_nodes = lax.optimization_barrier((value, grad_nodes))
    total = spread(value, core)
    return (grad_nodes, grad_edges, *total)


def solution(mesh):
    rows = P(("nodes", "rep"), None)
    flat = P(("nodes", "rep"))
    return jax.shard_map(
        shards,
        mesh=mesh,
        in_specs=(rows, rows, rows, rows, flat, flat, P("nodes", None, None)) + (P(),) * 7,
        out_specs=(rows, rows, P(), P(), P(), P()),
        check_vma=False,
    )
```

```python
import functools
import math

import jax
import jax.numpy as jnp
from jax import lax
from jax.experimental import pallas as pl
from jax.experimental.pallas import tpu as pltpu
from jax.sharding import PartitionSpec as P

EPS = 1e-05
bf16 = jnp.bfloat16
f32 = jnp.float32


def swapped(array):
    pairs = [(i, 1 - i) for i in range(2)]
    return lax.ppermute(array, "rep", pairs)


def mat_mul(left, right):
    return jnp.dot(left, right, preferred_element_type=f32)


def mat_tn(left, right):
    return lax.dot_general(left, right, (((0,), (0,)), ((), ())), preferred_element_type=f32)


def mat_nt(left, right):
    return lax.dot_general(left, right, (((1,), (1,)), ((), ())), preferred_element_type=f32)


def split_two(value):
    high = lax.reduce_precision(value, 8, 7)
    return high.astype(bf16), (value - high).astype(bf16)


def silu_slope(value):
    sigmoid_v = jax.nn.sigmoid(value)
    return sigmoid_v * (1.0 + value * (1.0 - sigmoid_v))


def norm_forward(value):
    centred = value - jnp.mean(value, axis=-1, keepdims=True)
    inverse = lax.rsqrt(jnp.mean(centred * centred, axis=-1, keepdims=True) + EPS)
    return (centred * inverse, inverse)


def norm_backward(grad_hat, normed, inverse):
    return inverse * (
        grad_hat
        - jnp.mean(grad_hat, axis=-1, keepdims=True)
        - normed * jnp.mean(grad_hat * normed, axis=-1, keepdims=True)
    )


def one_hot(index, width):
    return (index[:, None] == lax.broadcasted_iota(jnp.int32, (1, width), 1)).astype(bf16)


def groups(sizes):
    ny, nz, nx = sizes

    def device(y, z, x, r):
        return ((y * nz + z) * nx + x) * 2 + r

    def along_x(r):
        return [[device(y, z, x, r) for x in range(nx)] for y in range(ny) for z in range(nz)]

    def along_y(r):
        return [[device(y, z, x, r) for y in range(ny)] for x in range(nx) for z in range(nz)]

    last = [[device(y, z, x, r) for z in range(nz)] for y in range(ny) for x in range(nx) for r in range(2)]
    return along_x(0) + along_y(1), along_y(0) + along_x(1), last


STAGES = groups((4, 8, 4))


def exchange(array, stage):
    return lax.all_to_all(array, ("nodes", "rep"), 0, 0, tiled=True, axis_index_groups=stage)


def summed(value, stage):
    count = len(stage[0])
    blocks = exchange(value.reshape(count, value.shape[0] // count, value.shape[1]), stage)
    return jnp.sum(blocks.astype(f32), axis=0).astype(bf16)


def gathered(value, stage):
    count = len(stage[0])
    blocks = exchange(jnp.broadcast_to(value[None], (count, *value.shape)), stage)
    return blocks.reshape(count * value.shape[0], value.shape[1])


def reduced(value):
    for stage in STAGES:
        value = summed(value, stage)
    return value


def spread(value, core):
    for stage in STAGES[::-1]:
        value = gathered(value, stage)
    width = value.shape[1]
    sizes = [3 * width, width, 2 * width, width]
    return place(swapped(value), 1 - core, sizes, place(value, core, sizes))


def place_kernel(sizes, core_ref, half_ref, *refs):
    outs, sems = refs[-1 - len(sizes) : -1], refs[-1]
    core = core_ref[0]
    copies = []
    half = half_ref.shape[1] // 2
    for out, rows in zip(outs, sizes):
        for block in range(rows // (2 * half)):
            start = len(copies) * half
            row = pl.multiple_of(block * 2 * half + core * half, half)
            copies.append(
                pltpu.make_async_copy(
                    half_ref.at[pl.ds(start, half), :],
                    out.at[pl.ds(row, half), :],
                    sems.at[len(copies)],
                )
            )
    for copy in copies:
        copy.start()
    for copy in copies:
        copy.wait()


def place(half, core, sizes, outs=()):
    blocks = sum(sizes) // half.shape[1]
    anywhere = pl.BlockSpec(memory_space=pl.ANY)
    return pl.pallas_call(
        functools.partial(place_kernel, sizes),
        out_shape=[jax.ShapeDtypeStruct((rows, half.shape[1]), half.dtype) for rows in sizes],
        in_specs=[pl.BlockSpec(memory_space=pltpu.SMEM), pl.BlockSpec(memory_space=pltpu.VMEM)]
        + [anywhere] * len(outs),
        out_specs=[anywhere] * len(sizes),
        scratch_shapes=[pltpu.SemaphoreType.DMA((blocks,))],
        input_output_aliases={2 + k: k for k in range(len(outs))},
        name="place",
    )(core.astype(jnp.int32).reshape(1), half, *outs)


def by_lane(index, count):
    return (index == lax.broadcasted_iota(jnp.int32, (index.shape[0], count), 1)).astype(bf16)


LANES = 128


def column(square_ref, count):
    turned = jnp.transpose(square_ref[...])
    return jnp.concatenate([turned[:, k : k + 1] for k in range(count // LANES)], 0)


def line(square_ref, count):
    return jnp.concatenate([square_ref[k : k + 1] for k in range(count // LANES)], 1)


def in_square(index):
    return jnp.pad(index.reshape(-1, LANES), ((0, LANES - index.shape[0] // LANES), (0, 0)))


def by_row(index, count):
    return (index == lax.broadcasted_iota(jnp.int32, (count, index.shape[1]), 0)).astype(bf16)


def in_two(value):
    high = value.astype(bf16)
    return high, (value - high.astype(f32)).astype(bf16)


def silu_parts(value):
    sigmoid_v = 1.0 / (1.0 + jnp.exp(-value))
    return value * sigmoid_v, sigmoid_v * (1.0 + value * (1.0 - sigmoid_v))


def forward_kernel(
    known_ref, local_ref, sender_ref, receiver_ref, mine_ref, theirs_ref, w_in_ref, w_out_ref, gain_ref,
    offset_ref, send_ref, slope_ref, hidden_ref, normed_ref, inverse_ref, totals_ref, table_ref,
):
    edges, width = known_ref.shape
    ghosts = mine_ref.shape[0]
    table_ref[:ghosts] = mine_ref[...]
    table_ref[ghosts:] = theirs_ref[...]
    count = totals_ref.shape[0]
    index = column(sender_ref, edges) - count
    rows = mat_mul(by_lane(index, 2 * ghosts), table_ref[...])
    send_rows = (local_ref[...].astype(f32) + rows).astype(bf16)
    send_ref[...] = send_rows
    pre_act = known_ref[...] + mat_mul(send_rows, w_in_ref[width : 2 * width])
    hidden, slope = silu_parts(pre_act)
    slope_ref[...] = slope
    hidden = hidden.astype(bf16)
    hidden_ref[...] = hidden
    normed, inverse = norm_forward(mat_mul(hidden, w_out_ref[...]))
    normed_ref[...] = normed
    inverse_ref[...] = jnp.broadcast_to(inverse, inverse_ref.shape)
    high, low = in_two(normed * gain_ref[...] + offset_ref[...])
    pick = by_row(line(receiver_ref, edges), count)
    totals_ref[...] = mat_mul(pick, high) + mat_mul(pick, low)


def backward_kernel(
    partial_ref, other_ref, part_ref, node_cot_ref, w_node_in_ref, w_node_out_ref, node_gain_ref,
    cot_ref, slope_ref, normed_ref, inverse_ref,
    receiver_ref, sender_ref, w_out_ref, gain_ref,
    theirs_ref, mine_ref, grad_act_ref, grad_out_ref,
    totals_ref, node_hidden_ref, node_act_ref, node_out_ref,
    totals_grad_ref,
):
    width = cot_ref.shape[1]
    rows = part_ref.shape[0]
    own = rows // 2
    ghosts = mine_ref.shape[0]
    totals = jnp.concatenate(
        [partial_ref[:own] + other_ref[own:], partial_ref[own:] + other_ref[:own]], 0
    ).astype(bf16)
    node_pre = mat_mul(part_ref[...], w_node_in_ref[:width]) + mat_mul(
        totals, w_node_in_ref[width:]
    )
    hidden, slope = silu_parts(node_pre)
    hidden = hidden.astype(bf16)
    normed, inverse = norm_forward(mat_mul(hidden, w_node_out_ref[...]))
    grad_out = norm_backward(
        node_cot_ref[...].astype(f32) * node_gain_ref[...], normed, inverse
    ).astype(bf16)
    grad_act = (mat_nt(grad_out, w_node_out_ref[...]) * slope).astype(bf16)
    totals_grad_ref[...] = mat_nt(grad_act, w_node_in_ref[width:]).astype(bf16)
    totals_ref[...] = totals[:own]
    node_hidden_ref[...] = hidden[:own]
    node_act_ref[...] = grad_act[:own]
    node_out_ref[...] = grad_out[:own]

    edges = cot_ref.shape[0]
    message_grad = cot_ref[...].astype(f32) + mat_mul(
        by_lane(column(receiver_ref, edges), rows), totals_grad_ref[...]
    )
    grad_out = norm_backward(
        message_grad * gain_ref[...], normed_ref[...], inverse_ref[:, :1]
    ).astype(bf16)
    grad_out_ref[...] = grad_out
    grad_act_ref[...] = (mat_nt(grad_out, w_out_ref[...]) * slope_ref[...]).astype(bf16)
    index = line(sender_ref, edges)
    theirs_ref[...] = mat_mul(by_row(index - rows - ghosts, ghosts), grad_act_ref[...]).astype(bf16)
    mine_ref[...] = mat_mul(by_row(index - rows, ghosts), grad_act_ref[...])


def weights_kernel(
    core_ref, edge_ref, send_ref, recv_ref, hidden_ref, part_ref, totals_ref, node_hidden_ref,
    grad_act_ref, grad_out_ref, node_act_ref, node_out_ref,
    receiver_ref, sender_ref, node_cot_ref, w_node_in_ref,
    kept_ref, local_ref, recv_sum_ref, direct_ref, *sent_refs_and_block,
    edge_scale, node_scale,
):
    *sent_refs, block_ref = sent_refs_and_block
    width = edge_ref.shape[1]
    half = width // 2
    core = core_ref[0]
    own = totals_ref.shape[0]
    products = [
        (edge_ref[...], grad_act_ref[...], edge_scale),
        (send_ref[...], grad_act_ref[...], edge_scale),
        (recv_ref[...], grad_act_ref[...], edge_scale),
        (hidden_ref[...], grad_out_ref[...], edge_scale),
        (part_ref[:own], node_act_ref[...], node_scale),
        (totals_ref[...], node_act_ref[...], node_scale),
        (node_hidden_ref[...], node_out_ref[...], node_scale),
    ]
    for k, (left, right, scale) in enumerate(products):
        block_ref[...] = mat_tn(left, right) * scale
        mine = block_ref[pl.ds(pl.multiple_of(core * half, half), half), :]
        other = block_ref[pl.ds(pl.multiple_of((1 - core) * half, half), half), :]
        kept_ref[k * half : (k + 1) * half] = mine.astype(bf16)
        other = other.astype(bf16)
        size = sent_refs[0].shape[0]
        start = k * half
        while start < (k + 1) * half:
            stop = min((start // size + 1) * size, (k + 1) * half)
            sent_refs[start // size][start % size : start % size + stop - start] = other[
                start - k * half : stop - k * half
            ]
            start = stop

    rows, edges = part_ref.shape[0], edge_ref.shape[0]
    local_ref[...] = mat_mul(by_row(line(sender_ref, edges), rows), grad_act_ref[...])
    recv_sum_ref[...] = mat_mul(by_row(line(receiver_ref, edges), rows), grad_act_ref[...])
    direct_ref[...] = mat_nt(node_act_ref[...], w_node_in_ref[:width]) + node_cot_ref[...].astype(f32)


def pair_kernel(kept_ref, *refs):
    *got_refs, out_ref = refs
    rows = got_refs[0].shape[0]
    for k, got_ref in enumerate(got_refs):
        at = slice(k * rows, (k + 1) * rows)
        out_ref[at] = (kept_ref[at].astype(f32) + got_ref[...].astype(f32)).astype(bf16)


def run(kernel, name, arguments, results, scratch=(), scalars=0, flops=0):
    vmem = pl.BlockSpec(memory_space=pltpu.VMEM)
    return pl.pallas_call(
        kernel,
        in_specs=[pl.BlockSpec(memory_space=pltpu.SMEM)] * scalars
        + [vmem] * (len(arguments) - scalars),
        out_specs=[vmem] * len(results),
        out_shape=[jax.ShapeDtypeStruct(*result) for result in results],
        scratch_shapes=list(scratch),
        compiler_params=pltpu.CompilerParams(vmem_limit_bytes=60 * 1024 * 1024),
        cost_estimate=pl.CostEstimate(
            flops=flops, transcendentals=0, bytes_accessed=8 * 1024 * 1024
        ),
        name=name,
    )(*arguments)


def shards(
    node_latent,
    edge_saved,
    node_cot,
    edge_cot,
    senders,
    receivers,
    ghost_rows,
    w_edge_in,
    w_edge_out,
    edge_gain,
    edge_offset,
    w_node_in,
    w_node_out,
    node_gain,
):
    width = node_latent.shape[1]
    own = node_latent.shape[0]
    rows = 2 * own
    core = lax.axis_index("rep")
    slots = ghost_rows.shape[2] // 2
    parts = ghost_rows.shape[1]
    ghosts = parts * slots

    def local_row(index):
        moved = index - core * own
        return jnp.where(moved < 0, moved + rows, moved)

    partition = jnp.concatenate([node_latent, swapped(node_latent)], 0)
    lists = lax.dynamic_slice_in_dim(ghost_rows[0], core * slots, slots, 1).reshape(-1)
    pick_ghost = one_hot(local_row(lists), rows)
    outgoing = mat_mul(pick_ghost, partition).astype(bf16).reshape(parts, slots, width)
    outgoing, senders, receivers = lax.optimization_barrier((outgoing, senders, receivers))
    arrived = lax.all_to_all(outgoing, "nodes", 0, 0, tiled=True)

    edge_latent = swapped(edge_saved)
    node_cots = jnp.concatenate([node_cot, swapped(node_cot)], 0)
    edges = senders.shape[0]
    receiver = local_row(receivers)
    slot = senders - rows
    side = ((slot >> 2) & 1) ^ core
    sender = jnp.where(
        slot >= 0,
        rows + side * ghosts + (slot >> 3) * slots + (slot & (slots - 1)),
        local_row(senders),
    )
    sender_square, receiver_square = in_square(sender), in_square(receiver)
    square = 2 * edges * width * width
    pick_recv = one_hot(receiver, rows)
    pick_local = one_hot(jnp.where(slot >= 0, -1, sender), rows)
    recv_rows = mat_mul(pick_recv, partition).astype(bf16)
    local_rows = mat_mul(pick_local, partition).astype(bf16)
    known = mat_mul(edge_latent, w_edge_in[:width]) + mat_mul(recv_rows, w_edge_in[2 * width :])
    (
        arrived, known, local_rows, recv_rows, sender_square, receiver_square, node_cots
    ) = lax.optimization_barrier(
        (arrived, known, local_rows, recv_rows, sender_square, receiver_square, node_cots)
    )
    arrived = arrived.reshape(ghosts, width)
    send_rows, edge_slope, edge_hidden, edge_normed, edge_inverse, partial = run(
        forward_kernel,
        "forward",
        [
            known,
            local_rows,
            sender_square,
            receiver_square,
            arrived,
            swapped(arrived),
            w_edge_in,
            w_edge_out,
            edge_gain[None],
            edge_offset[None],
        ],
        [
            ((edges, width), bf16),
            ((edges, width), f32),
            ((edges, width), bf16),
            ((edges, width), f32),
            ((edges, 128), f32),
            ((rows, width), f32),
        ],
        [pltpu.VMEM((2 * ghosts, width), bf16)],
        flops=6 * square,
    )
    device_count = lax.axis_size("nodes") * lax.axis_size("rep")
    edge_scale = 1.0 / math.sqrt(edges * device_count)
    node_scale = 1.0 / math.sqrt(own * device_count)
    (
        theirs, mine, grad_act, grad_out,
        totals, node_hidden, node_act, node_out,
    ) = run(
        backward_kernel,
        "backward",
        [
            partial,
            swapped(partial),
            partition,
            node_cots,
            w_node_in,
            w_node_out,
            node_gain[None],
            edge_cot,
            edge_slope,
            edge_normed,
            edge_inverse,
            receiver_square,
            sender_square,
            w_edge_out,
            edge_gain[None],
        ],
        [
            ((ghosts, width), bf16),
            ((ghosts, width), f32),
            ((edges, width), bf16),
            ((edges, width), bf16),
        ]
        + [((own, width), bf16)] * 4,
        [pltpu.VMEM((rows, width), bf16)],
        flops=8 * square,
    )
    paired = (mine + swapped(theirs).astype(f32)).astype(bf16)
    paired, grad_act = lax.optimization_barrier((paired, grad_act))
    returned = lax.all_to_all(paired.reshape(parts, slots, width), "nodes", 0, 0, tiled=True)

    kept, local_sum, recv_sum, direct_grad, *sent = run(
        functools.partial(weights_kernel, edge_scale=edge_scale, node_scale=node_scale),
        "weights",
        [
            core.astype(jnp.int32).reshape(1),
            edge_latent,
            send_rows,
            recv_rows,
            edge_hidden,
            partition,
            totals,
            node_hidden,
            grad_act,
            grad_out,
            node_act,
            node_out,
            receiver_square,
            sender_square,
            node_cot,
            w_node_in,
        ],
        [((7 * width // 2, width), bf16)]
        + [((rows, width), f32)] * 2
        + [((own, width), f32)]
        + [((7 * width // 8, width), bf16)] * 4,
        [pltpu.VMEM((width, width), f32)],
        scalars=1,
        flops=6 * square,
    )

    got = [swapped(block) for block in sent]
    kept, got, returned = lax.optimization_barrier((kept, got, returned))
    value = reduced(
        run(pair_kernel, "pair", [kept, *got], [(kept.shape, bf16)], flops=kept.size)[0]
    )
    send_high, send_low = split_two(local_sum + mat_tn(pick_ghost, returned.reshape(ghosts, width)))
    recv_high, recv_low = split_two(recv_sum)
    a2, a3 = w_edge_in[width : 2 * width], w_edge_in[2 * width :]
    row_grad = (
        mat_nt(recv_high, a3) + mat_nt(recv_low, a3) + mat_nt(send_high, a2) + mat_nt(send_low, a2)
    )
    own_grad = row_grad[:own] + swapped(row_grad[own:])
    grad_nodes = (own_grad + direct_grad).astype(bf16)

    grad_edges = (edge_cot.astype(f32) + mat_nt(grad_act, w_edge_in[:width])).astype(bf16)
    value, grad_nodes, grad_edges = lax.optimization_barrier((value, grad_nodes, grad_edges))
    total = spread(value, core)
    return (grad_nodes, grad_edges, *total)


def solution(mesh):
    rows = P(("nodes", "rep"), None)
    flat = P(("nodes", "rep"))
    return jax.shard_map(
        shards,
        mesh=mesh,
        in_specs=(rows, rows, rows, rows, flat, flat, P("nodes", None, None)) + (P(),) * 7,
        out_specs=(rows, rows, P(), P(), P(), P()),
        check_vma=False,
    )
```

```python
import functools
import math

import jax
import jax.numpy as jnp
from jax import lax
from jax.experimental import pallas as pl
from jax.experimental.pallas import tpu as pltpu
from jax.sharding import PartitionSpec as P

EPS = 1e-05
bf16 = jnp.bfloat16
f32 = jnp.float32


def swapped(array):
    pairs = [(i, 1 - i) for i in range(2)]
    return lax.ppermute(array, "rep", pairs)


def mat_mul(left, right):
    return jnp.dot(left, right, preferred_element_type=f32)


def mat_tn(left, right):
    return lax.dot_general(left, right, (((0,), (0,)), ((), ())), preferred_element_type=f32)


def mat_nt(left, right):
    return lax.dot_general(left, right, (((1,), (1,)), ((), ())), preferred_element_type=f32)


def split_two(value):
    high = lax.reduce_precision(value, 8, 7)
    return high.astype(bf16), (value - high).astype(bf16)


def silu_slope(value):
    sigmoid_v = jax.nn.sigmoid(value)
    return sigmoid_v * (1.0 + value * (1.0 - sigmoid_v))


def norm_forward(value):
    centred = value - jnp.mean(value, axis=-1, keepdims=True)
    inverse = lax.rsqrt(jnp.mean(centred * centred, axis=-1, keepdims=True) + EPS)
    return (centred * inverse, inverse)


def norm_backward(grad_hat, normed, inverse):
    return inverse * (
        grad_hat
        - jnp.mean(grad_hat, axis=-1, keepdims=True)
        - normed * jnp.mean(grad_hat * normed, axis=-1, keepdims=True)
    )


def one_hot(index, width):
    return (index[:, None] == lax.broadcasted_iota(jnp.int32, (1, width), 1)).astype(bf16)


def groups(sizes):
    ny, nz, nx = sizes

    def device(y, z, x, r):
        return ((y * nz + z) * nx + x) * 2 + r

    def along_x(r):
        return [[device(y, z, x, r) for x in range(nx)] for y in range(ny) for z in range(nz)]

    def along_y(r):
        return [[device(y, z, x, r) for y in range(ny)] for x in range(nx) for z in range(nz)]

    last = [[device(y, z, x, r) for z in range(nz)] for y in range(ny) for x in range(nx) for r in range(2)]
    return along_x(0) + along_y(1), along_y(0) + along_x(1), last


STAGES = groups((4, 8, 4))


def exchange(array, stage):
    return lax.all_to_all(array, ("nodes", "rep"), 0, 0, tiled=True, axis_index_groups=stage)


def summed(value, stage):
    count = len(stage[0])
    blocks = exchange(value.reshape(count, value.shape[0] // count, value.shape[1]), stage)
    return jnp.sum(blocks.astype(f32), axis=0).astype(bf16)


def gathered(value, stage):
    count = len(stage[0])
    blocks = exchange(jnp.broadcast_to(value[None], (count, *value.shape)), stage)
    return blocks.reshape(count * value.shape[0], value.shape[1])


def reduced(value):
    for stage in STAGES:
        value = summed(value, stage)
    return value


def spread(value, core):
    for stage in STAGES[::-1]:
        value = gathered(value, stage)
    width = value.shape[1]
    sizes = [3 * width, width, 2 * width, width]
    return place(swapped(value), 1 - core, sizes, place(value, core, sizes))


def place_kernel(sizes, core_ref, half_ref, *refs):
    outs, sems = refs[-1 - len(sizes) : -1], refs[-1]
    core = core_ref[0]
    copies = []
    half = half_ref.shape[1] // 2
    for out, rows in zip(outs, sizes):
        for block in range(rows // (2 * half)):
            start = len(copies) * half
            row = pl.multiple_of(block * 2 * half + core * half, half)
            copies.append(
                pltpu.make_async_copy(
                    half_ref.at[pl.ds(start, half), :],
                    out.at[pl.ds(row, half), :],
                    sems.at[len(copies)],
                )
            )
    for copy in copies:
        copy.start()
    for copy in copies:
        copy.wait()


def place(half, core, sizes, outs=()):
    blocks = sum(sizes) // half.shape[1]
    anywhere = pl.BlockSpec(memory_space=pl.ANY)
    return pl.pallas_call(
        functools.partial(place_kernel, sizes),
        out_shape=[jax.ShapeDtypeStruct((rows, half.shape[1]), half.dtype) for rows in sizes],
        in_specs=[pl.BlockSpec(memory_space=pltpu.SMEM), pl.BlockSpec(memory_space=pltpu.VMEM)]
        + [anywhere] * len(outs),
        out_specs=[anywhere] * len(sizes),
        scratch_shapes=[pltpu.SemaphoreType.DMA((blocks,))],
        input_output_aliases={2 + k: k for k in range(len(outs))},
        compiler_params=pltpu.CompilerParams(vmem_limit_bytes=4 * 1024 * 1024),
        name="place",
    )(core.astype(jnp.int32).reshape(1), half, *outs)


def by_lane(index, count):
    return (index == lax.broadcasted_iota(jnp.int32, (index.shape[0], count), 1)).astype(bf16)


LANES = 128


def column(square_ref, count):
    turned = jnp.transpose(square_ref[...])
    return jnp.concatenate([turned[:, k : k + 1] for k in range(count // LANES)], 0)


def line(square_ref, count):
    return jnp.concatenate([square_ref[k : k + 1] for k in range(count // LANES)], 1)


def in_square(index):
    return jnp.pad(index.reshape(-1, LANES), ((0, LANES - index.shape[0] // LANES), (0, 0)))


def by_row(index, count):
    return (index == lax.broadcasted_iota(jnp.int32, (count, index.shape[1]), 0)).astype(bf16)


def in_two(value):
    high = value.astype(bf16)
    return high, (value - high.astype(f32)).astype(bf16)


def silu_parts(value):
    sigmoid_v = 1.0 / (1.0 + jnp.exp(-value))
    return value * sigmoid_v, sigmoid_v * (1.0 + value * (1.0 - sigmoid_v))


def forward_kernel(
    known_ref, local_ref, sender_ref, receiver_ref, mine_ref, theirs_ref, w_in_ref, w_out_ref, gain_ref,
    offset_ref, send_ref, slope_ref, hidden_ref, normed_ref, inverse_ref, totals_ref, table_ref,
):
    edges, width = known_ref.shape
    ghosts = mine_ref.shape[0]
    table_ref[:ghosts] = mine_ref[...]
    table_ref[ghosts:] = theirs_ref[...]
    count = totals_ref.shape[0]
    index = column(sender_ref, edges) - count
    rows = mat_mul(by_lane(index, 2 * ghosts), table_ref[...])
    send_rows = (local_ref[...].astype(f32) + rows).astype(bf16)
    send_ref[...] = send_rows
    pre_act = known_ref[...] + mat_mul(send_rows, w_in_ref[width : 2 * width])
    hidden, slope = silu_parts(pre_act)
    slope_ref[...] = slope
    hidden = hidden.astype(bf16)
    hidden_ref[...] = hidden
    normed, inverse = norm_forward(mat_mul(hidden, w_out_ref[...]))
    normed_ref[...] = normed
    inverse_ref[...] = jnp.broadcast_to(inverse, inverse_ref.shape)
    high, low = in_two(normed * gain_ref[...] + offset_ref[...])
    pick = by_row(line(receiver_ref, edges), count)
    totals_ref[...] = mat_mul(pick, high) + mat_mul(pick, low)


def backward_kernel(
    partial_ref, other_ref, part_ref, node_cot_ref, w_node_in_ref, w_node_out_ref, node_gain_ref,
    cot_ref, slope_ref, normed_ref, inverse_ref,
    receiver_ref, sender_ref, w_out_ref, gain_ref,
    theirs_ref, mine_ref, grad_act_ref, grad_out_ref,
    totals_ref, node_hidden_ref, node_act_ref, node_out_ref,
    totals_grad_ref,
):
    width = cot_ref.shape[1]
    rows = part_ref.shape[0]
    own = rows // 2
    ghosts = mine_ref.shape[0]
    totals = jnp.concatenate(
        [partial_ref[:own] + other_ref[own:], partial_ref[own:] + other_ref[:own]], 0
    ).astype(bf16)
    node_pre = mat_mul(part_ref[...], w_node_in_ref[:width]) + mat_mul(
        totals, w_node_in_ref[width:]
    )
    hidden, slope = silu_parts(node_pre)
    hidden = hidden.astype(bf16)
    normed, inverse = norm_forward(mat_mul(hidden, w_node_out_ref[...]))
    grad_out = norm_backward(
        node_cot_ref[...].astype(f32) * node_gain_ref[...], normed, inverse
    ).astype(bf16)
    grad_act = (mat_nt(grad_out, w_node_out_ref[...]) * slope).astype(bf16)
    totals_grad_ref[...] = mat_nt(grad_act, w_node_in_ref[width:]).astype(bf16)
    totals_ref[...] = totals[:own]
    node_hidden_ref[...] = hidden[:own]
    node_act_ref[...] = grad_act[:own]
    node_out_ref[...] = grad_out[:own]

    edges = cot_ref.shape[0]
    message_grad = cot_ref[...].astype(f32) + mat_mul(
        by_lane(column(receiver_ref, edges), rows), totals_grad_ref[...]
    )
    grad_out = norm_backward(
        message_grad * gain_ref[...], normed_ref[...], inverse_ref[:, :1]
    ).astype(bf16)
    grad_out_ref[...] = grad_out
    grad_act_ref[...] = (mat_nt(grad_out, w_out_ref[...]) * slope_ref[...]).astype(bf16)
    index = line(sender_ref, edges)
    theirs_ref[...] = mat_mul(by_row(index - rows - ghosts, ghosts), grad_act_ref[...]).astype(bf16)
    mine_ref[...] = mat_mul(by_row(index - rows, ghosts), grad_act_ref[...])


def weights_kernel(
    core_ref, edge_ref, send_ref, recv_ref, hidden_ref, part_ref, totals_ref, node_hidden_ref,
    grad_act_ref, grad_out_ref, node_act_ref, node_out_ref,
    receiver_ref, sender_ref, node_cot_ref, w_node_in_ref,
    kept_ref, local_ref, recv_sum_ref, direct_ref, *sent_refs_and_block,
    edge_scale, node_scale,
):
    *sent_refs, block_ref = sent_refs_and_block
    width = edge_ref.shape[1]
    half = width // 2
    core = core_ref[0]
    own = totals_ref.shape[0]
    products = [
        (edge_ref[...], grad_act_ref[...], edge_scale),
        (send_ref[...], grad_act_ref[...], edge_scale),
        (recv_ref[...], grad_act_ref[...], edge_scale),
        (hidden_ref[...], grad_out_ref[...], edge_scale),
        (part_ref[:own], node_act_ref[...], node_scale),
        (totals_ref[...], node_act_ref[...], node_scale),
        (node_hidden_ref[...], node_out_ref[...], node_scale),
    ]
    for k, (left, right, scale) in enumerate(products):
        block_ref[...] = mat_tn(left, right) * scale
        mine = block_ref[pl.ds(pl.multiple_of(core * half, half), half), :]
        other = block_ref[pl.ds(pl.multiple_of((1 - core) * half, half), half), :]
        kept_ref[k * half : (k + 1) * half] = mine.astype(bf16)
        other = other.astype(bf16)
        size = sent_refs[0].shape[0]
        start = k * half
        while start < (k + 1) * half:
            stop = min((start // size + 1) * size, (k + 1) * half)
            sent_refs[start // size][start % size : start % size + stop - start] = other[
                start - k * half : stop - k * half
            ]
            start = stop

    rows, edges = part_ref.shape[0], edge_ref.shape[0]
    local_ref[...] = mat_mul(by_row(line(sender_ref, edges), rows), grad_act_ref[...])
    recv_sum_ref[...] = mat_mul(by_row(line(receiver_ref, edges), rows), grad_act_ref[...])
    direct_ref[...] = mat_nt(node_act_ref[...], w_node_in_ref[:width]) + node_cot_ref[...].astype(f32)


def pair_kernel(kept_ref, *refs):
    *got_refs, out_ref = refs
    rows = got_refs[0].shape[0]
    for k, got_ref in enumerate(got_refs):
        at = slice(k * rows, (k + 1) * rows)
        out_ref[at] = (kept_ref[at].astype(f32) + got_ref[...].astype(f32)).astype(bf16)


def run(kernel, name, arguments, results, scratch=(), scalars=0, flops=0, room=22):
    vmem = pl.BlockSpec(memory_space=pltpu.VMEM)
    return pl.pallas_call(
        kernel,
        in_specs=[pl.BlockSpec(memory_space=pltpu.SMEM)] * scalars
        + [vmem] * (len(arguments) - scalars),
        out_specs=[vmem] * len(results),
        out_shape=[jax.ShapeDtypeStruct(*result) for result in results],
        scratch_shapes=list(scratch),
        compiler_params=pltpu.CompilerParams(vmem_limit_bytes=room * 1024 * 1024),
        cost_estimate=pl.CostEstimate(
            flops=flops, transcendentals=0, bytes_accessed=8 * 1024 * 1024
        ),
        name=name,
    )(*arguments)


def shards(
    node_latent,
    edge_saved,
    node_cot,
    edge_cot,
    senders,
    receivers,
    ghost_rows,
    w_edge_in,
    w_edge_out,
    edge_gain,
    edge_offset,
    w_node_in,
    w_node_out,
    node_gain,
):
    width = node_latent.shape[1]
    own = node_latent.shape[0]
    rows = 2 * own
    core = lax.axis_index("rep")
    slots = ghost_rows.shape[2] // 2
    parts = ghost_rows.shape[1]
    ghosts = parts * slots

    def local_row(index):
        moved = index - core * own
        return jnp.where(moved < 0, moved + rows, moved)

    partition = jnp.concatenate([node_latent, swapped(node_latent)], 0)
    lists = lax.dynamic_slice_in_dim(ghost_rows[0], core * slots, slots, 1).reshape(-1)
    pick_ghost = one_hot(local_row(lists), rows)
    outgoing = mat_mul(pick_ghost, partition).astype(bf16).reshape(parts, slots, width)
    outgoing, senders, receivers = lax.optimization_barrier((outgoing, senders, receivers))
    arrived = lax.all_to_all(outgoing, "nodes", 0, 0, tiled=True)

    edge_latent = swapped(edge_saved)
    node_cots = jnp.concatenate([node_cot, swapped(node_cot)], 0)
    edges = senders.shape[0]
    receiver = local_row(receivers)
    slot = senders - rows
    side = ((slot >> 2) & 1) ^ core
    sender = jnp.where(
        slot >= 0,
        rows + side * ghosts + (slot >> 3) * slots + (slot & (slots - 1)),
        local_row(senders),
    )
    sender_square, receiver_square = in_square(sender), in_square(receiver)
    square = 2 * edges * width * width
    pick_recv = one_hot(receiver, rows)
    pick_local = one_hot(jnp.where(slot >= 0, -1, sender), rows)
    recv_rows = mat_mul(pick_recv, partition).astype(bf16)
    local_rows = mat_mul(pick_local, partition).astype(bf16)
    known = mat_mul(edge_latent, w_edge_in[:width]) + mat_mul(recv_rows, w_edge_in[2 * width :])
    (
        arrived, known, local_rows, recv_rows, sender_square, receiver_square, node_cots
    ) = lax.optimization_barrier(
        (arrived, known, local_rows, recv_rows, sender_square, receiver_square, node_cots)
    )
    arrived = arrived.reshape(ghosts, width)
    send_rows, edge_slope, edge_hidden, edge_normed, edge_inverse, partial = run(
        forward_kernel,
        "forward",
        [
            known,
            local_rows,
            sender_square,
            receiver_square,
            arrived,
            swapped(arrived),
            w_edge_in,
            w_edge_out,
            edge_gain[None],
            edge_offset[None],
        ],
        [
            ((edges, width), bf16),
            ((edges, width), f32),
            ((edges, width), bf16),
            ((edges, width), f32),
            ((edges, 128), f32),
            ((rows, width), f32),
        ],
        [pltpu.VMEM((2 * ghosts, width), bf16)],
        flops=6 * square,
    )
    device_count = lax.axis_size("nodes") * lax.axis_size("rep")
    edge_scale = 1.0 / math.sqrt(edges * device_count)
    node_scale = 1.0 / math.sqrt(own * device_count)
    (
        theirs, mine, grad_act, grad_out,
        totals, node_hidden, node_act, node_out,
    ) = run(
        backward_kernel,
        "backward",
        [
            partial,
            swapped(partial),
            partition,
            node_cots,
            w_node_in,
            w_node_out,
            node_gain[None],
            edge_cot,
            edge_slope,
            edge_normed,
            edge_inverse,
            receiver_square,
            sender_square,
            w_edge_out,
            edge_gain[None],
        ],
        [
            ((ghosts, width), bf16),
            ((ghosts, width), f32),
            ((edges, width), bf16),
            ((edges, width), bf16),
        ]
        + [((own, width), bf16)] * 4,
        [pltpu.VMEM((rows, width), bf16)],
        flops=8 * square,
    )
    paired = (mine + swapped(theirs).astype(f32)).astype(bf16)
    paired, grad_act = lax.optimization_barrier((paired, grad_act))
    returned = lax.all_to_all(paired.reshape(parts, slots, width), "nodes", 0, 0, tiled=True)

    kept, local_sum, recv_sum, direct_grad, *sent = run(
        functools.partial(weights_kernel, edge_scale=edge_scale, node_scale=node_scale),
        "weights",
        [
            core.astype(jnp.int32).reshape(1),
            edge_latent,
            send_rows,
            recv_rows,
            edge_hidden,
            partition,
            totals,
            node_hidden,
            grad_act,
            grad_out,
            node_act,
            node_out,
            receiver_square,
            sender_square,
            node_cot,
            w_node_in,
        ],
        [((7 * width // 2, width), bf16)]
        + [((rows, width), f32)] * 2
        + [((own, width), f32)]
        + [((7 * width // 8, width), bf16)] * 4,
        [pltpu.VMEM((width, width), f32)],
        scalars=1,
        flops=6 * square,
    )

    got = [swapped(block) for block in sent]
    kept, got, returned = lax.optimization_barrier((kept, got, returned))
    value = reduced(
        run(pair_kernel, "pair", [kept, *got], [(kept.shape, bf16)], flops=kept.size, room=6)[0]
    )
    send_high, send_low = split_two(local_sum + mat_tn(pick_ghost, returned.reshape(ghosts, width)))
    recv_high, recv_low = split_two(recv_sum)
    a2, a3 = w_edge_in[width : 2 * width], w_edge_in[2 * width :]
    row_grad = (
        mat_nt(recv_high, a3) + mat_nt(recv_low, a3) + mat_nt(send_high, a2) + mat_nt(send_low, a2)
    )
    own_grad = row_grad[:own] + swapped(row_grad[own:])
    grad_nodes = (own_grad + direct_grad).astype(bf16)

    grad_edges = (edge_cot.astype(f32) + mat_nt(grad_act, w_edge_in[:width])).astype(bf16)
    value, grad_nodes, grad_edges = lax.optimization_barrier((value, grad_nodes, grad_edges))
    total = spread(value, core)
    return (grad_nodes, grad_edges, *total)


def solution(mesh):
    rows = P(("nodes", "rep"), None)
    flat = P(("nodes", "rep"))
    return jax.shard_map(
        shards,
        mesh=mesh,
        in_specs=(rows, rows, rows, rows, flat, flat, P("nodes", None, None)) + (P(),) * 7,
        out_specs=(rows, rows, P(), P(), P(), P()),
        check_vma=False,
    )
```

```python
import functools
import math

import jax
import jax.numpy as jnp
from jax import lax
from jax.experimental import pallas as pl
from jax.experimental.pallas import tpu as pltpu
from jax.sharding import PartitionSpec as P

EPS = 1e-05
bf16 = jnp.bfloat16
f32 = jnp.float32


def swapped(array):
    pairs = [(i, 1 - i) for i in range(2)]
    return lax.ppermute(array, "rep", pairs)


def mat_mul(left, right):
    return jnp.dot(left, right, preferred_element_type=f32)


def mat_tn(left, right):
    return lax.dot_general(left, right, (((0,), (0,)), ((), ())), preferred_element_type=f32)


def mat_nt(left, right):
    return lax.dot_general(left, right, (((1,), (1,)), ((), ())), preferred_element_type=f32)


def split_two(value):
    high = lax.reduce_precision(value, 8, 7)
    return high.astype(bf16), (value - high).astype(bf16)


def silu_slope(value):
    sigmoid_v = jax.nn.sigmoid(value)
    return sigmoid_v * (1.0 + value * (1.0 - sigmoid_v))


def norm_forward(value):
    centred = value - jnp.mean(value, axis=-1, keepdims=True)
    inverse = lax.rsqrt(jnp.mean(centred * centred, axis=-1, keepdims=True) + EPS)
    return (centred * inverse, inverse)


def norm_backward(grad_hat, normed, inverse):
    return inverse * (
        grad_hat
        - jnp.mean(grad_hat, axis=-1, keepdims=True)
        - normed * jnp.mean(grad_hat * normed, axis=-1, keepdims=True)
    )


def one_hot(index, width):
    return (index[:, None] == lax.broadcasted_iota(jnp.int32, (1, width), 1)).astype(bf16)


def groups(sizes):
    ny, nz, nx = sizes

    def device(y, z, x, r):
        return ((y * nz + z) * nx + x) * 2 + r

    def along_x(r):
        return [[device(y, z, x, r) for x in range(nx)] for y in range(ny) for z in range(nz)]

    def along_y(r):
        return [[device(y, z, x, r) for y in range(ny)] for x in range(nx) for z in range(nz)]

    last = [[device(y, z, x, r) for z in range(nz)] for y in range(ny) for x in range(nx) for r in range(2)]
    return along_x(0) + along_y(1), along_y(0) + along_x(1), last


STAGES = groups((4, 8, 4))


def exchange(array, stage):
    return lax.all_to_all(array, ("nodes", "rep"), 0, 0, tiled=True, axis_index_groups=stage)


def summed(value, stage):
    count = len(stage[0])
    blocks = exchange(value.reshape(count, value.shape[0] // count, value.shape[1]), stage)
    return jnp.sum(blocks.astype(f32), axis=0).astype(bf16)


def gathered(value, stage):
    count = len(stage[0])
    blocks = exchange(jnp.broadcast_to(value[None], (count, *value.shape)), stage)
    return blocks.reshape(count * value.shape[0], value.shape[1])


def reduced(value):
    for stage in STAGES:
        value = summed(value, stage)
    return value


def spread(value, core):
    for stage in STAGES[::-1]:
        value = gathered(value, stage)
    width = value.shape[1]
    sizes = [3 * width, width, 2 * width, width]
    return place(swapped(value), 1 - core, sizes, place(value, core, sizes))


def place_kernel(sizes, core_ref, half_ref, *refs):
    outs, sems = refs[-1 - len(sizes) : -1], refs[-1]
    core = core_ref[0]
    copies = []
    half = half_ref.shape[1] // 2
    for out, rows in zip(outs, sizes):
        for block in range(rows // (2 * half)):
            start = len(copies) * half
            row = pl.multiple_of(block * 2 * half + core * half, half)
            copies.append(
                pltpu.make_async_copy(
                    half_ref.at[pl.ds(start, half), :],
                    out.at[pl.ds(row, half), :],
                    sems.at[len(copies)],
                )
            )
    for copy in copies:
        copy.start()
    for copy in copies:
        copy.wait()


def place(half, core, sizes, outs=()):
    blocks = sum(sizes) // half.shape[1]
    anywhere = pl.BlockSpec(memory_space=pl.ANY)
    return pl.pallas_call(
        functools.partial(place_kernel, sizes),
        out_shape=[jax.ShapeDtypeStruct((rows, half.shape[1]), half.dtype) for rows in sizes],
        in_specs=[pl.BlockSpec(memory_space=pltpu.SMEM), pl.BlockSpec(memory_space=pltpu.VMEM)]
        + [anywhere] * len(outs),
        out_specs=[anywhere] * len(sizes),
        scratch_shapes=[pltpu.SemaphoreType.DMA((blocks,))],
        input_output_aliases={2 + k: k for k in range(len(outs))},
        name="place",
    )(core.astype(jnp.int32).reshape(1), half, *outs)


def by_lane(index, count):
    return (index == lax.broadcasted_iota(jnp.int32, (index.shape[0], count), 1)).astype(bf16)


LANES = 128


def column(square_ref, count):
    turned = jnp.transpose(square_ref[...])
    return jnp.concatenate([turned[:, k : k + 1] for k in range(count // LANES)], 0)


def line(square_ref, count):
    return jnp.concatenate([square_ref[k : k + 1] for k in range(count // LANES)], 1)


def in_square(index):
    return jnp.pad(index.reshape(-1, LANES), ((0, LANES - index.shape[0] // LANES), (0, 0)))


def by_row(index, count):
    return (index == lax.broadcasted_iota(jnp.int32, (count, index.shape[1]), 0)).astype(bf16)


def in_two(value):
    high = value.astype(bf16)
    return high, (value - high.astype(f32)).astype(bf16)


def silu_parts(value):
    sigmoid_v = 1.0 / (1.0 + jnp.exp(-value))
    return value * sigmoid_v, sigmoid_v * (1.0 + value * (1.0 - sigmoid_v))


def forward_kernel(
    known_ref, local_ref, sender_ref, receiver_ref, mine_ref, theirs_ref, w_in_ref, w_out_ref, gain_ref,
    offset_ref, send_ref, slope_ref, hidden_ref, normed_ref, inverse_ref, totals_ref, table_ref,
):
    edges, width = known_ref.shape
    ghosts = mine_ref.shape[0]
    table_ref[:ghosts] = mine_ref[...]
    table_ref[ghosts:] = theirs_ref[...]
    count = totals_ref.shape[0]
    index = column(sender_ref, edges) - count
    rows = mat_mul(by_lane(index, 2 * ghosts), table_ref[...])
    send_rows = (local_ref[...].astype(f32) + rows).astype(bf16)
    send_ref[...] = send_rows
    pre_act = known_ref[...] + mat_mul(send_rows, w_in_ref[width : 2 * width])
    hidden, slope = silu_parts(pre_act)
    slope_ref[...] = slope
    hidden = hidden.astype(bf16)
    hidden_ref[...] = hidden
    normed, inverse = norm_forward(mat_mul(hidden, w_out_ref[...]))
    normed_ref[...] = normed
    inverse_ref[...] = jnp.broadcast_to(inverse, inverse_ref.shape)
    high, low = in_two(normed * gain_ref[...] + offset_ref[...])
    pick = by_row(line(receiver_ref, edges), count)
    totals_ref[...] = mat_mul(pick, high) + mat_mul(pick, low)


def backward_kernel(
    partial_ref, other_ref, part_ref, node_cot_ref, w_node_in_ref, w_node_out_ref, node_gain_ref,
    cot_ref, slope_ref, normed_ref, inverse_ref,
    receiver_ref, sender_ref, w_out_ref, gain_ref,
    theirs_ref, mine_ref, grad_act_ref, grad_out_ref,
    totals_ref, node_hidden_ref, node_act_ref, node_out_ref,
    totals_grad_ref,
):
    width = cot_ref.shape[1]
    rows = part_ref.shape[0]
    own = rows // 2
    ghosts = mine_ref.shape[0]
    totals = jnp.concatenate(
        [partial_ref[:own] + other_ref[own:], partial_ref[own:] + other_ref[:own]], 0
    ).astype(bf16)
    node_pre = mat_mul(part_ref[...], w_node_in_ref[:width]) + mat_mul(
        totals, w_node_in_ref[width:]
    )
    hidden, slope = silu_parts(node_pre)
    hidden = hidden.astype(bf16)
    normed, inverse = norm_forward(mat_mul(hidden, w_node_out_ref[...]))
    grad_out = norm_backward(
        node_cot_ref[...].astype(f32) * node_gain_ref[...], normed, inverse
    ).astype(bf16)
    grad_act = (mat_nt(grad_out, w_node_out_ref[...]) * slope).astype(bf16)
    totals_grad_ref[...] = mat_nt(grad_act, w_node_in_ref[width:]).astype(bf16)
    totals_ref[...] = totals[:own]
    node_hidden_ref[...] = hidden[:own]
    node_act_ref[...] = grad_act[:own]
    node_out_ref[...] = grad_out[:own]

    edges = cot_ref.shape[0]
    message_grad = cot_ref[...].astype(f32) + mat_mul(
        by_lane(column(receiver_ref, edges), rows), totals_grad_ref[...]
    )
    grad_out = norm_backward(
        message_grad * gain_ref[...], normed_ref[...], inverse_ref[:, :1]
    ).astype(bf16)
    grad_out_ref[...] = grad_out
    grad_act_ref[...] = (mat_nt(grad_out, w_out_ref[...]) * slope_ref[...]).astype(bf16)
    index = line(sender_ref, edges)
    theirs_ref[...] = mat_mul(by_row(index - rows - ghosts, ghosts), grad_act_ref[...]).astype(bf16)
    mine_ref[...] = mat_mul(by_row(index - rows, ghosts), grad_act_ref[...])


def weights_kernel(
    core_ref, edge_ref, send_ref, recv_ref, hidden_ref, part_ref, totals_ref, node_hidden_ref,
    grad_act_ref, grad_out_ref, node_act_ref, node_out_ref,
    receiver_ref, sender_ref, node_cot_ref, w_node_in_ref,
    kept_ref, local_ref, recv_sum_ref, direct_ref, *sent_refs_and_block,
    edge_scale, node_scale,
):
    *sent_refs, block_ref = sent_refs_and_block
    width = edge_ref.shape[1]
    half = width // 2
    core = core_ref[0]
    own = totals_ref.shape[0]
    products = [
        (edge_ref[...], grad_act_ref[...], edge_scale),
        (send_ref[...], grad_act_ref[...], edge_scale),
        (recv_ref[...], grad_act_ref[...], edge_scale),
        (hidden_ref[...], grad_out_ref[...], edge_scale),
        (part_ref[:own], node_act_ref[...], node_scale),
        (totals_ref[...], node_act_ref[...], node_scale),
        (node_hidden_ref[...], node_out_ref[...], node_scale),
    ]
    for k, (left, right, scale) in enumerate(products):
        block_ref[...] = mat_tn(left, right) * scale
        mine = block_ref[pl.ds(pl.multiple_of(core * half, half), half), :]
        other = block_ref[pl.ds(pl.multiple_of((1 - core) * half, half), half), :]
        kept_ref[k * half : (k + 1) * half] = mine.astype(bf16)
        other = other.astype(bf16)
        size = sent_refs[0].shape[0]
        start = k * half
        while start < (k + 1) * half:
            stop = min((start // size + 1) * size, (k + 1) * half)
            sent_refs[start // size][start % size : start % size + stop - start] = other[
                start - k * half : stop - k * half
            ]
            start = stop

    rows, edges = part_ref.shape[0], edge_ref.shape[0]
    local_ref[...] = mat_mul(by_row(line(sender_ref, edges), rows), grad_act_ref[...])
    recv_sum_ref[...] = mat_mul(by_row(line(receiver_ref, edges), rows), grad_act_ref[...])
    direct_ref[...] = mat_nt(node_act_ref[...], w_node_in_ref[:width]) + node_cot_ref[...].astype(f32)


def pair_kernel(kept_ref, *refs):
    *got_refs, out_ref = refs
    rows = got_refs[0].shape[0]
    for k, got_ref in enumerate(got_refs):
        at = slice(k * rows, (k + 1) * rows)
        out_ref[at] = (kept_ref[at].astype(f32) + got_ref[...].astype(f32)).astype(bf16)


def run(kernel, name, arguments, results, scratch=(), scalars=0, flops=0, room=60):
    vmem = pl.BlockSpec(memory_space=pltpu.VMEM)
    return pl.pallas_call(
        kernel,
        in_specs=[pl.BlockSpec(memory_space=pltpu.SMEM)] * scalars
        + [vmem] * (len(arguments) - scalars),
        out_specs=[vmem] * len(results),
        out_shape=[jax.ShapeDtypeStruct(*result) for result in results],
        scratch_shapes=list(scratch),
        compiler_params=pltpu.CompilerParams(vmem_limit_bytes=room * 1024 * 1024),
        cost_estimate=pl.CostEstimate(
            flops=flops, transcendentals=0, bytes_accessed=8 * 1024 * 1024
        ),
        name=name,
    )(*arguments)


def shards(
    node_latent,
    edge_saved,
    node_cot,
    edge_cot,
    senders,
    receivers,
    ghost_rows,
    w_edge_in,
    w_edge_out,
    edge_gain,
    edge_offset,
    w_node_in,
    w_node_out,
    node_gain,
):
    width = node_latent.shape[1]
    own = node_latent.shape[0]
    rows = 2 * own
    core = lax.axis_index("rep")
    slots = ghost_rows.shape[2] // 2
    parts = ghost_rows.shape[1]
    ghosts = parts * slots

    def local_row(index):
        moved = index - core * own
        return jnp.where(moved < 0, moved + rows, moved)

    partition = jnp.concatenate([node_latent, swapped(node_latent)], 0)
    lists = lax.dynamic_slice_in_dim(ghost_rows[0], core * slots, slots, 1).reshape(-1)
    pick_ghost = one_hot(local_row(lists), rows)
    outgoing = mat_mul(pick_ghost, partition).astype(bf16).reshape(parts, slots, width)
    outgoing, senders, receivers = lax.optimization_barrier((outgoing, senders, receivers))
    arrived = lax.all_to_all(outgoing, "nodes", 0, 0, tiled=True)

    edge_latent = swapped(edge_saved)
    node_cots = jnp.concatenate([node_cot, swapped(node_cot)], 0)
    edges = senders.shape[0]
    receiver = local_row(receivers)
    slot = senders - rows
    side = ((slot >> 2) & 1) ^ core
    sender = jnp.where(
        slot >= 0,
        rows + side * ghosts + (slot >> 3) * slots + (slot & (slots - 1)),
        local_row(senders),
    )
    sender_square, receiver_square = in_square(sender), in_square(receiver)
    square = 2 * edges * width * width
    pick_recv = one_hot(receiver, rows)
    pick_local = one_hot(jnp.where(slot >= 0, -1, sender), rows)
    recv_rows = mat_mul(pick_recv, partition).astype(bf16)
    local_rows = mat_mul(pick_local, partition).astype(bf16)
    known = mat_mul(edge_latent, w_edge_in[:width]) + mat_mul(recv_rows, w_edge_in[2 * width :])
    (
        arrived, known, local_rows, recv_rows, sender_square, receiver_square, node_cots
    ) = lax.optimization_barrier(
        (arrived, known, local_rows, recv_rows, sender_square, receiver_square, node_cots)
    )
    arrived = arrived.reshape(ghosts, width)
    send_rows, edge_slope, edge_hidden, edge_normed, edge_inverse, partial = run(
        forward_kernel,
        "forward",
        [
            known,
            local_rows,
            sender_square,
            receiver_square,
            arrived,
            swapped(arrived),
            w_edge_in,
            w_edge_out,
            edge_gain[None],
            edge_offset[None],
        ],
        [
            ((edges, width), bf16),
            ((edges, width), f32),
            ((edges, width), bf16),
            ((edges, width), f32),
            ((edges, 128), f32),
            ((rows, width), f32),
        ],
        [pltpu.VMEM((2 * ghosts, width), bf16)],
        flops=6 * square,
        room=22,
    )
    device_count = lax.axis_size("nodes") * lax.axis_size("rep")
    edge_scale = 1.0 / math.sqrt(edges * device_count)
    node_scale = 1.0 / math.sqrt(own * device_count)
    (
        theirs, mine, grad_act, grad_out,
        totals, node_hidden, node_act, node_out,
    ) = run(
        backward_kernel,
        "backward",
        [
            partial,
            swapped(partial),
            partition,
            node_cots,
            w_node_in,
            w_node_out,
            node_gain[None],
            edge_cot,
            edge_slope,
            edge_normed,
            edge_inverse,
            receiver_square,
            sender_square,
            w_edge_out,
            edge_gain[None],
        ],
        [
            ((ghosts, width), bf16),
            ((ghosts, width), f32),
            ((edges, width), bf16),
            ((edges, width), bf16),
        ]
        + [((own, width), bf16)] * 4,
        [pltpu.VMEM((rows, width), bf16)],
        flops=8 * square,
        room=22,
    )
    paired = (mine + swapped(theirs).astype(f32)).astype(bf16)
    paired, grad_act = lax.optimization_barrier((paired, grad_act))
    returned = lax.all_to_all(paired.reshape(parts, slots, width), "nodes", 0, 0, tiled=True)

    kept, local_sum, recv_sum, direct_grad, *sent = run(
        functools.partial(weights_kernel, edge_scale=edge_scale, node_scale=node_scale),
        "weights",
        [
            core.astype(jnp.int32).reshape(1),
            edge_latent,
            send_rows,
            recv_rows,
            edge_hidden,
            partition,
            totals,
            node_hidden,
            grad_act,
            grad_out,
            node_act,
            node_out,
            receiver_square,
            sender_square,
            node_cot,
            w_node_in,
        ],
        [((7 * width // 2, width), bf16)]
        + [((rows, width), f32)] * 2
        + [((own, width), f32)]
        + [((7 * width // 8, width), bf16)] * 4,
        [pltpu.VMEM((width, width), f32)],
        scalars=1,
        flops=6 * square,
    )

    got = [swapped(block) for block in sent]
    kept, got, returned = lax.optimization_barrier((kept, got, returned))
    value = reduced(
        run(pair_kernel, "pair", [kept, *got], [(kept.shape, bf16)], flops=kept.size)[0]
    )
    send_high, send_low = split_two(local_sum + mat_tn(pick_ghost, returned.reshape(ghosts, width)))
    recv_high, recv_low = split_two(recv_sum)
    a2, a3 = w_edge_in[width : 2 * width], w_edge_in[2 * width :]
    row_grad = (
        mat_nt(recv_high, a3) + mat_nt(recv_low, a3) + mat_nt(send_high, a2) + mat_nt(send_low, a2)
    )
    own_grad = row_grad[:own] + swapped(row_grad[own:])
    grad_nodes = (own_grad + direct_grad).astype(bf16)

    grad_edges = (edge_cot.astype(f32) + mat_nt(grad_act, w_edge_in[:width])).astype(bf16)
    value, grad_nodes, grad_edges = lax.optimization_barrier((value, grad_nodes, grad_edges))
    total = spread(value, core)
    return (grad_nodes, grad_edges, *total)


def solution(mesh):
    rows = P(("nodes", "rep"), None)
    flat = P(("nodes", "rep"))
    return jax.shard_map(
        shards,
        mesh=mesh,
        in_specs=(rows, rows, rows, rows, flat, flat, P("nodes", None, None)) + (P(),) * 7,
        out_specs=(rows, rows, P(), P(), P(), P()),
        check_vma=False,
    )
```
